32 devices in a mesh: leaf: 32 (over z, y, x, core).
Axes of the slice: x: 2, y: 2, z: 4, core: 2. Of those that a mesh axis runs over, the one named last changes fastest.
Arguments:
- near_blocks: bfloat16 [64, 26, 256, 256], P('leaf'), may hold values from -0.0582 to 0.0582
- diag_blocks: bfloat16 [64, 256, 256], P('leaf'), as said below
- bases: bfloat16 [64, 256, 256], P('leaf'), as said below
- leaf_nbrs: int32 [64, 26], P('leaf'), may hold values from -1 to 63, as said below
- parent_nbrs: int32 [8, 5], replicated, may hold values from 0 to 7, as said below
Outputs:
- leaf_factor: float32 [64, 128, 128], P('leaf')
- leaf_panel: float32 [64, 128, 128], P('leaf')
- merged: float32 [64, 5, 128, 1024], P('leaf')
- parent_block: float32 [8192, 1024], P('leaf')
The draws below stay inside these ranges and needn't reach their ends.
Inputs may be any that keep to these rules, and one draw needn't show every extreme that they name: `leaf_nbrs`: row i lists distinct leaves j with j != i and |j - i| <= 16; live entries come first and -1 fills the rest; every row has at least 13 live entries and some row has all 26. `parent_nbrs`: row P begins with P itself, followed by the other 4 parents nearest to P in numbering, distinct, equally near ones in any order. `diag_blocks`: each block is symmetric positive definite. `bases`: each basis is an orthogonal matrix rounded to bfloat16.
All inputs are finite; a program needn't handle non-finite values.
Results may differ from the reference program's by a relative error of at most 0.001.
The reference program's roundings to bfloat16 on the way count: a program that leaves them out, or rounds other values in their place, can miss the bound.
Values may be sent and summed in bfloat16 or wider, within the bound.
A program may use at most 128 MiB of HBM per device.

```python
import jax
import jax.numpy as jnp
from jax import lax

LR = 256
RANK = 128
NB = 26
REACH = 16
CHILDREN = 8
LEAVES = 64
PARENTS = 8
PNB = 5


def draw_near_blocks(key, part):
    base_key = jax.random.fold_in(key, 53)

    def one_leaf(leaf_index):
        leaf_key = jax.random.fold_in(base_key, leaf_index)
        values = jnp.clip(0.013 * jax.random.normal(leaf_key, (NB, LR, LR), jnp.float32), -0.058, 0.058)
        return values.astype(jnp.bfloat16)
    return lax.map(one_leaf, jnp.arange(LEAVES, dtype=jnp.int32))


def draw_diag_blocks(key, part):
    key_scale, key_mix = jax.random.split(jax.random.fold_in(key, 11))
    scales = jnp.exp(jax.random.uniform(key_scale, (LEAVES, LR), jnp.float32, jnp.log(1.0), jnp.log(4.0)))

    def one_leaf(leaf_index):
        leaf_key = jax.random.fold_in(key_mix, leaf_index)
        mixing = jax.random.normal(leaf_key, (LR, LR), jnp.float32)
        gram = jnp.dot(mixing, mixing.T, precision=lax.Precision.HIGHEST) / LR
        return 0.5 * (gram + gram.T)
    grams = lax.map(one_leaf, jnp.arange(LEAVES, dtype=jnp.int32))
    blocks = grams + scales[:, :, None] * jnp.eye(LR, dtype=jnp.float32)[None]
    return blocks.astype(jnp.bfloat16)


def draw_bases(key, part):
    source = jax.random.normal(jax.random.fold_in(key, 23), (LEAVES, LR, LR), jnp.float32)
    orthogonal, upper_part = jnp.linalg.qr(source)
    return orthogonal.astype(jnp.bfloat16)


def draw_leaf_nbrs(key, part):
    base_key = jax.random.fold_in(key, 37)
    key_rank, key_count, key_full = jax.random.split(base_key, 3)
    offsets = jnp.concatenate([jnp.arange(-REACH, 0), jnp.arange(1, REACH + 1)]).astype(jnp.int32)
    row_keys = jax.random.split(key_rank, LEAVES)
    row_ranks = jax.vmap(lambda row_key: jax.random.permutation(row_key, 2 * REACH))(row_keys).astype(jnp.int32)
    leaves = jnp.arange(LEAVES, dtype=jnp.int32)
    targets = leaves[:, None] + offsets[None, :]
    in_range = (targets >= 0) & (targets < LEAVES)
    scores = in_range.astype(jnp.int32) * 1024 + row_ranks
    top_scores, picked_slots = lax.top_k(scores, NB)
    chosen = leaves[:, None] + offsets[picked_slots]
    counts = jax.random.randint(key_count, (LEAVES,), 13, NB + 1)
    full_leaf = jax.random.randint(key_full, (), REACH, LEAVES - REACH)
    counts = jnp.where(leaves == full_leaf, NB, counts)
    slot_ids = jnp.arange(NB, dtype=jnp.int32)[None, :]
    is_live = (slot_ids < counts[:, None]) & (top_scores >= 1024)
    return jnp.where(is_live, chosen, -1).astype(jnp.int32)


def draw_parent_nbrs(key, part):
    row_ranks = jax.random.permutation(jax.random.fold_in(key, 41), PARENTS).astype(jnp.int32)
    parents = jnp.arange(PARENTS, dtype=jnp.int32)
    distance = jnp.abs(parents[:, None] - parents[None, :])
    scores = -distance * 4096 + row_ranks[None, :]
    top_scores, picked = lax.top_k(scores, PNB)
    return picked.astype(jnp.int32)


def setup_inputs(seed: int = 0) -> dict:
    key_of = jax.random.split(jax.random.key(seed), 6)
    near_blocks = draw_near_blocks(jax.random.fold_in(key_of[5], 71), 0)
    diag_blocks = draw_diag_blocks(jax.random.fold_in(key_of[5], 71), 0)
    bases = draw_bases(jax.random.fold_in(key_of[5], 71), 0)
    leaf_nbrs = draw_leaf_nbrs(jax.random.fold_in(key_of[5], 71), 0)
    parent_nbrs = draw_parent_nbrs(jax.random.fold_in(key_of[5], 71), 0)
    return dict(near_blocks=near_blocks, diag_blocks=diag_blocks, bases=bases, leaf_nbrs=leaf_nbrs, parent_nbrs=parent_nbrs)


highest = lax.Precision.HIGHEST

def lower_solve(lower_factor, right_side):
    return lax.linalg.triangular_solve(lower_factor, right_side, left_side=True, lower=True)

def back_solve(lower_factor, right_side):
    return lax.linalg.triangular_solve(lower_factor, right_side, left_side=True, lower=True, transpose_a=True)

def factor_leaf(block, basis):
    basis_wide = basis.astype(jnp.float32)
    half_proj = jnp.dot(basis_wide.T, block.astype(jnp.float32), precision=highest).astype(jnp.bfloat16)
    half_proj = lax.optimization_barrier(half_proj).astype(jnp.float32)
    dense = jnp.dot(half_proj, basis_wide, precision=highest)
    redundant = LR - RANK
    lower_factor = jnp.linalg.cholesky(dense[:redundant, :redundant])
    panel_rows = lower_solve(lower_factor, dense[:redundant, redundant:])
    skeleton = dense[redundant:, redundant:] - jnp.dot(panel_rows.T, panel_rows, precision=highest)
    shift_rows = back_solve(lower_factor, panel_rows)
    return (lower_factor, panel_rows, skeleton, shift_rows)

def reference(near_blocks, diag_blocks, bases, leaf_nbrs, parent_nbrs):
    redundant = LR - RANK
    leaf_factor, leaf_panel, skeleton, shift_wide = jax.vmap(factor_leaf)(diag_blocks, bases)
    leaf_shift = lax.optimization_barrier(shift_wide.astype(jnp.bfloat16)).astype(jnp.float32)

    def leaf_row(leaf_index):
        neighbours = leaf_nbrs[leaf_index]
        is_live = neighbours >= 0
        clipped = jnp.maximum(neighbours, 0)
        basis_wide = bases[leaf_index].astype(jnp.float32)
        half_proj = jnp.einsum('ba,nbc->nac', basis_wide, near_blocks[leaf_index].astype(jnp.float32), precision=highest).astype(jnp.bfloat16)
        half_proj = lax.optimization_barrier(half_proj).astype(jnp.float32)
        coupled = jnp.einsum('nac,ncb->nab', half_proj, bases[clipped].astype(jnp.float32), precision=highest)
        own_shift = leaf_shift[leaf_index]
        first_term = jnp.einsum('ka,nkb->nab', own_shift, coupled[:, :redundant, redundant:], precision=highest)
        second_term = jnp.einsum('nak,nkb->nab', coupled[:, redundant:, :redundant], leaf_shift[clipped], precision=highest)
        near_schur = jnp.where(is_live[:, None, None], coupled[:, redundant:, redundant:] - first_term - second_term, jnp.float32(0.0))
        parent = leaf_index // CHILDREN
        position = leaf_index % CHILDREN
        targets = parent_nbrs[parent]
        children = jnp.arange(CHILDREN, dtype=jnp.int32)
        slot_hits = is_live[None, None, :] & (clipped[None, None, :] // CHILDREN == targets[:, None, None]) & (clipped[None, None, :] % CHILDREN == children[None, :, None])
        self_hit = (targets[:, None] == parent) & (children[None, :] == position)
        parent_rows = jnp.einsum('qbn,nxy->qxby', slot_hits.astype(jnp.float32), near_schur, precision=highest)
        parent_rows = parent_rows + self_hit.astype(jnp.float32)[:, None, :, None] * skeleton[leaf_index][None, :, None, :]
        parent_rows = parent_rows.reshape(PNB, RANK, CHILDREN * RANK)
        return (parent_rows, parent_rows[0])
    merged, diagonal_rows = lax.map(leaf_row, jnp.arange(LEAVES, dtype=jnp.int32))
    blocks = diagonal_rows.reshape(PARENTS, CHILDREN * RANK, CHILDREN * RANK)
    symmetric = 0.5 * (blocks + jnp.transpose(blocks, (0, 2, 1)))
    return (leaf_factor, leaf_panel, merged, symmetric.reshape(LEAVES * RANK, CHILDREN * RANK))
```

```python
import functools

import jax
import jax.numpy as jnp
from jax import lax
from jax.experimental import pallas as pl
from jax.experimental.pallas import tpu as pltpu
from jax.sharding import PartitionSpec as P

RANK = 128
REACH = 16
CHILDREN = 8
PANEL = 32
MESH = pl.DeviceIdType.MESH
highest = lax.Precision.HIGHEST


def matmul(a, b):
    return jnp.dot(a, b, preferred_element_type=jnp.float32)


def matmul_t(a, b, precision=None):
    return lax.dot_general(
        a, b, (((0,), (0,)), ((), ())), preferred_element_type=jnp.float32, precision=precision
    )


def factor_kernel(diag, bases, factor, panel, skeleton, shift, shift_t2, bases_t, work, rows):
    per_device, leaf_rows = bases.shape[0], bases.shape[1]
    red = leaf_rows - RANK
    wide = 2 * red + RANK
    row_id = lax.broadcasted_iota(jnp.int32, (red, red), 0)
    col_id = lax.broadcasted_iota(jnp.int32, (red, red), 1)
    low_corner = []
    for leaf in range(per_device):
        basis = bases[leaf]
        basis_t = basis.T
        bases_t[leaf] = basis_t
        half = matmul(basis_t, diag[leaf]).astype(jnp.bfloat16)
        dense = matmul(half, basis)
        top = dense[:red, :red]
        work[leaf, :, :red] = 0.5 * (top + top.T)
        work[leaf, :, red : red + RANK] = dense[:red, red:]
        work[leaf, :, red + RANK :] = (row_id == col_id).astype(jnp.float32)
        low_corner.append(dense[red:, red:])
    sub = lax.broadcasted_iota(jnp.int32, (PANEL, 1), 0)
    for start in range(0, red, PANEL):
        strips = [work[leaf, start : start + PANEL, :] for leaf in range(per_device)]
        for k in range(PANEL):
            for leaf in range(per_device):
                strip = strips[leaf]
                column = strip[:, start + k : start + k + 1]
                ratio = jnp.where(sub > k, column / column[k : k + 1], 0.0)
                strips[leaf] = strip - ratio * strip[k : k + 1, :]
        lane = lax.broadcasted_iota(jnp.int32, (PANEL, wide), 1)
        line = lax.broadcasted_iota(jnp.int32, (PANEL, wide), 0)
        for leaf in range(per_device):
            strip = strips[leaf]
            pivots = jnp.sum(jnp.where(lane == line + start, strip, 0.0), axis=1, keepdims=True)
            strip = strip * (1.0 / jnp.sqrt(pivots))
            rows[leaf, start : start + PANEL, :] = strip
            if start + PANEL < red:
                work[leaf] = work[leaf] - matmul_t(strip[:, :red], strip, highest)
    for leaf in range(per_device):
        upper = jnp.where(col_id >= row_id, rows[leaf, :, :red], 0.0)
        factor[leaf] = upper.T
        solved = rows[leaf, :, red : red + RANK]
        panel[leaf] = solved
        inverse = jnp.where(col_id <= row_id, rows[leaf, :, red + RANK :], 0.0)
        skeleton[leaf] = low_corner[leaf] - matmul_t(solved, solved, highest)
        moved = matmul_t(inverse, solved, highest)
        shift[leaf] = moved.astype(jnp.bfloat16)
        turned = moved.T.astype(jnp.bfloat16)
        shift_t2[leaf, :, :red] = turned
        shift_t2[leaf, :, red:] = turned


def window_kernel(
    chips, count, bases, shift, win_bases, win_shift, send, recv, pass_send, pass_recv, own_sem
):
    me = lax.axis_index("leaf")
    core = me % 2
    sibling = me + 1 - 2 * core
    offsets = [sign * step for step in range(chips, 0, -1) for sign in (1, -1)]
    pairs = ((bases, win_bases), (shift, win_shift))

    def inside(offset):
        other = me + 2 * offset
        return (other >= 0) & (other < count)

    barrier = pltpu.get_barrier_semaphore()
    pl.semaphore_signal(barrier, inc=1, device_id=(sibling,), device_id_type=MESH)
    for offset in offsets:

        @pl.when(inside(offset))
        def _(offset=offset):
            pl.semaphore_signal(barrier, inc=1, device_id=(me + 2 * offset,), device_id_type=MESH)

    peers = jnp.int32(1)
    for offset in offsets:
        peers = peers + inside(offset).astype(jnp.int32)
    pl.semaphore_wait(barrier, peers)

    def direct(kind, offset):
        source, window = pairs[kind]
        return pltpu.make_async_remote_copy(
            src_ref=source,
            dst_ref=window.at[2 * (chips - offset) + core],
            send_sem=send.at[kind, chips + offset],
            recv_sem=recv.at[kind, chips - offset],
            device_id=(me + 2 * offset,),
            device_id_type=MESH,
        )

    def arrival(kind, offset):
        source, window = pairs[kind]
        return pltpu.make_async_remote_copy(
            src_ref=source,
            dst_ref=window.at[2 * (chips + offset) + core],
            send_sem=send.at[kind, chips + offset],
            recv_sem=recv.at[kind, chips + offset],
            device_id=(sibling,),
            device_id_type=MESH,
        )

    def relay(kind, offset):
        source, window = pairs[kind]
        slot = 2 * (chips + offset) + core
        return pltpu.make_async_remote_copy(
            src_ref=source if offset == 0 else window.at[slot],
            dst_ref=window.at[slot],
            send_sem=pass_send.at[kind, chips + offset],
            recv_sem=pass_recv.at[kind, chips + offset],
            device_id=(sibling,),
            device_id_type=MESH,
        )

    def relayed(kind, offset):
        source, window = pairs[kind]
        slot = 2 * (chips + offset) + 1 - core
        return pltpu.make_async_remote_copy(
            src_ref=source,
            dst_ref=window.at[slot],
            send_sem=pass_send.at[kind, chips + offset],
            recv_sem=pass_recv.at[kind, chips + offset],
            device_id=(sibling,),
            device_id_type=MESH,
        )

    for kind in range(2):
        for offset in offsets:

            @pl.when(inside(offset))
            def _(kind=kind, offset=offset):
                direct(kind, offset).start()

        relay(kind, 0).start()
        source, window = pairs[kind]
        pltpu.make_async_copy(source, window.at[2 * chips + core], own_sem.at[kind]).start()

    for kind in range(2):
        for offset in offsets[::-1]:

            @pl.when(inside(offset))
            def _(kind=kind, offset=offset):
                arrival(kind, offset).wait_recv()
                relay(kind, offset).start()

    for kind in range(2):
        source, window = pairs[kind]
        pltpu.make_async_copy(source, window.at[2 * chips + core], own_sem.at[kind]).wait()
        relay(kind, 0).wait_send()
        relayed(kind, 0).wait_recv()
        for offset in offsets:

            @pl.when(inside(offset))
            def _(kind=kind, offset=offset):
                direct(kind, offset).wait_send()
                relay(kind, offset).wait_send()
                relayed(kind, offset).wait_recv()


def couple_kernel(
    chips,
    group,
    where,
    nbrs,
    parents,
    near,
    bases_t,
    shift_t2,
    skeleton,
    win_bases,
    win_shift,
    merged,
    diagonal,
):
    leaf, step = pl.program_id(0), pl.program_id(1)
    per_device = pl.num_programs(0)
    steps = pl.num_programs(1)
    red = bases_t.shape[1] - RANK
    me = where[0]
    number = me * per_device + leaf
    parent = number // CHILDREN
    targets = parents.shape[1]

    @pl.when(step == 0)
    def _():
        merged[...] = jnp.zeros_like(merged)
        place = pl.multiple_of((number % CHILDREN) * RANK, RANK)
        for q in range(targets):

            @pl.when(parents[parent, q] == parent)
            def _(q=q):
                merged[0, q, :, pl.ds(place, RANK)] = skeleton[0]

    @pl.when(nbrs[leaf, step * group] >= 0)
    def _():
        for k in range(group):
            other = nbrs[leaf, step * group + k]
            safe = jnp.where(other >= 0, other, number)
            owner = safe // per_device
            slot = (owner // 2 - me // 2 + chips) * 2 + owner % 2
            basis = win_bases[slot, safe % per_device]
            moved = win_shift[slot, safe % per_device]
            half = matmul(bases_t[0], near[0, k]).astype(jnp.bfloat16)
            right = matmul(half, basis[:, red:])
            left = matmul(half[red:], basis[:, :red])
            high = right[:red].astype(jnp.bfloat16)
            low = (right[:red] - high.astype(jnp.float32)).astype(jnp.bfloat16)
            first = matmul(shift_t2[0], jnp.concatenate([high, low], axis=0))
            high = left.astype(jnp.bfloat16)
            low = (left - high.astype(jnp.float32)).astype(jnp.bfloat16)
            second = matmul(
                jnp.concatenate([high, low], axis=1), jnp.concatenate([moved, moved], axis=0)
            )
            schur = right[red:] - first - second
            target = safe // CHILDREN
            q = jnp.int32(-1)
            for n in range(targets):
                q = jnp.where(parents[parent, n] == target, n, q)

            @pl.when((other >= 0) & (q >= 0))
            def _(schur=schur, q=q, safe=safe):
                place = pl.multiple_of((safe % CHILDREN) * RANK, RANK)
                merged[0, q, :, pl.ds(place, RANK)] = schur

    @pl.when(step == steps - 1)
    def _():
        diagonal[0] = merged[0, 0].astype(jnp.bfloat16)


def parent_kernel(size, own, diagonal, block, landed, send, recv):
    me = lax.axis_index("leaf")
    place = me % size
    base = me - place
    per_device, rank = own.shape[0], own.shape[2]
    width = per_device * rank
    barrier = pltpu.get_barrier_semaphore()
    for t in range(1, size):
        pl.semaphore_signal(
            barrier, inc=1, device_id=(base + (place + t) % size,), device_id_type=MESH
        )
    pl.semaphore_wait(barrier, size - 1)

    def copy(t):
        other = (place + t) % size
        return pltpu.make_async_remote_copy(
            src_ref=diagonal.at[:, :, pl.ds(pl.multiple_of(other * width, 128), width)],
            dst_ref=landed.at[size - t],
            send_sem=send.at[t],
            recv_sem=recv.at[size - t],
            device_id=(base + other,),
            device_id_type=MESH,
        )

    for t in range(1, size):
        copy(t).start()
    for t in range(size):
        other = (place + t) % size
        columns = pl.ds(pl.multiple_of(other * width, 128), width)
        mine = own[:, 0, :, columns].reshape(width, width)
        if t == 0:
            theirs = mine
        else:
            copy(size - t).wait_recv()
            theirs = landed[t].reshape(width, width).astype(jnp.float32)
        block[:, columns] = 0.5 * (mine + theirs.T)
    for t in range(1, size):
        copy(t).wait_send()


def local(count, near_blocks, diag_blocks, bases, leaf_nbrs, parent_nbrs):
    per_device, leaf_rows = bases.shape[0], bases.shape[1]
    red = leaf_rows - RANK
    slots = near_blocks.shape[1]
    targets = parent_nbrs.shape[1]
    span = REACH // per_device
    chips = (span + 1) // 2
    vmem = pl.BlockSpec(memory_space=pltpu.VMEM)
    anywhere = pl.BlockSpec(memory_space=pl.ANY)
    f32, bf16 = jnp.float32, jnp.bfloat16

    def out(shape, dtype):
        return jax.ShapeDtypeStruct(shape, dtype)

    factor, panel, skeleton, shift, shift_t2, bases_t = pl.pallas_call(
        factor_kernel,
        out_shape=(
            out((per_device, red, red), f32),
            out((per_device, red, RANK), f32),
            out((per_device, RANK, RANK), f32),
            out((per_device, red, RANK), bf16),
            out((per_device, RANK, 2 * red), bf16),
            out(bases.shape, bf16),
        ),
        in_specs=[vmem] * 2,
        out_specs=(vmem,) * 6,
        scratch_shapes=[
            pltpu.VMEM((per_device, red, 2 * red + RANK), f32),
            pltpu.VMEM((per_device, red, 2 * red + RANK), f32),
        ],
        name="factor",
    )(diag_blocks, bases)

    window = 2 * (2 * chips + 1)
    sems = pltpu.SemaphoreType.DMA((2, 2 * chips + 1))
    win_bases, win_shift = pl.pallas_call(
        functools.partial(window_kernel, chips, count),
        out_shape=(
            out((window,) + bases.shape, bf16),
            out((window,) + shift.shape, bf16),
        ),
        in_specs=[vmem] * 2,
        out_specs=(anywhere,) * 2,
        scratch_shapes=[sems, sems, sems, sems, pltpu.SemaphoreType.DMA((2,))],
        compiler_params=pltpu.CompilerParams(collective_id=0, has_side_effects=True),
        name="window",
    )(bases, shift)

    group = 2 if slots % 2 == 0 else 1
    where = lax.axis_index("leaf").astype(jnp.int32).reshape(1)

    def near_map(leaf, step, where, nbrs, parents):
        return leaf, jnp.where(nbrs[leaf, step * group] >= 0, step, 0), 0, 0

    def by_leaf(rank):
        return lambda leaf, step, *_: (leaf,) + (0,) * (rank - 1)

    merged, diagonal = pl.pallas_call(
        functools.partial(couple_kernel, chips, group),
        out_shape=(
            out((per_device, targets, RANK, CHILDREN * RANK), f32),
            out((per_device, RANK, CHILDREN * RANK), bf16),
        ),
        grid_spec=pltpu.PrefetchScalarGridSpec(
            num_scalar_prefetch=3,
            grid=(per_device, slots // group),
            in_specs=[
                pl.BlockSpec((1, group, leaf_rows, leaf_rows), near_map),
                pl.BlockSpec((1, leaf_rows, leaf_rows), by_leaf(3)),
                pl.BlockSpec((1, RANK, 2 * red), by_leaf(3)),
                pl.BlockSpec((1, RANK, RANK), by_leaf(3)),
                vmem,
                vmem,
            ],
            out_specs=(
                pl.BlockSpec((1, targets, RANK, CHILDREN * RANK), by_leaf(4)),
                pl.BlockSpec((1, RANK, CHILDREN * RANK), by_leaf(3)),
            ),
        ),
        compiler_params=pltpu.CompilerParams(
            dimension_semantics=("arbitrary", "arbitrary"), vmem_limit_bytes=48 << 20
        ),
        name="couple",
    )(where, leaf_nbrs, parent_nbrs, near_blocks, bases_t, shift_t2, skeleton, win_bases, win_shift)

    size = CHILDREN // per_device
    width = per_device * RANK
    parent_block = pl.pallas_call(
        functools.partial(parent_kernel, size),
        out_shape=out((width, CHILDREN * RANK), f32),
        grid=(1,),
        in_specs=[
            pl.BlockSpec((per_device, 1, RANK, CHILDREN * RANK), lambda i: (0, 0, 0, 0)),
            vmem,
        ],
        out_specs=vmem,
        scratch_shapes=[
            pltpu.VMEM((size, per_device, RANK, width), bf16),
            pltpu.SemaphoreType.DMA((size,)),
            pltpu.SemaphoreType.DMA((size,)),
        ],
        compiler_params=pltpu.CompilerParams(collective_id=1, has_side_effects=True),
        name="parent",
    )(merged, diagonal)
    return factor, panel, merged, parent_block


def solution(mesh):
    count = mesh.shape["leaf"]
    in_specs = (
        P("leaf", None, None, None),
        P("leaf", None, None),
        P("leaf", None, None),
        P("leaf", None),
        P(),
    )
    out_specs = (
        P("leaf", None, None),
        P("leaf", None, None),
        P("leaf", None, None, None),
        P("leaf", None),
    )
    return jax.shard_map(
        functools.partial(local, count),
        mesh=mesh,
        in_specs=in_specs,
        out_specs=out_specs,
        check_vma=False,
    )
```

```python
import functools

import jax
import jax.numpy as jnp
from jax import lax
from jax.experimental import pallas as pl
from jax.experimental.pallas import tpu as pltpu
from jax.sharding import PartitionSpec as P

RANK = 128
REACH = 16
CHILDREN = 8
PANEL = 32
MESH = pl.DeviceIdType.MESH
highest = lax.Precision.HIGHEST


def matmul(a, b):
    return jnp.dot(a, b, preferred_element_type=jnp.float32)


def matmul_t(a, b, precision=None):
    return lax.dot_general(
        a, b, (((0,), (0,)), ((), ())), preferred_element_type=jnp.float32, precision=precision
    )


def eliminate(diag, bases, factor, panel, skeleton, shift, shift_t2, bases_t, work, rows):
    per_device, leaf_rows = bases.shape[0], bases.shape[1]
    red = leaf_rows - RANK
    wide = 2 * red + RANK
    row_id = lax.broadcasted_iota(jnp.int32, (red, red), 0)
    col_id = lax.broadcasted_iota(jnp.int32, (red, red), 1)
    low_corner = []
    for leaf in range(per_device):
        basis = bases[leaf]
        basis_t = basis.T
        bases_t[leaf] = basis_t
        half = matmul(basis_t, diag[leaf]).astype(jnp.bfloat16)
        dense = matmul(half, basis)
        top = dense[:red, :red]
        work[leaf, :, :red] = 0.5 * (top + top.T)
        work[leaf, :, red : red + RANK] = dense[:red, red:]
        work[leaf, :, red + RANK :] = (row_id == col_id).astype(jnp.float32)
        low_corner.append(dense[red:, red:])
    sub = lax.broadcasted_iota(jnp.int32, (PANEL, 1), 0)
    for start in range(0, red, PANEL):
        strips = [work[leaf, start : start + PANEL, :] for leaf in range(per_device)]
        for k in range(PANEL):
            for leaf in range(per_device):
                strip = strips[leaf]
                column = strip[:, start + k : start + k + 1]
                ratio = jnp.where(sub > k, column / column[k : k + 1], 0.0)
                strips[leaf] = strip - ratio * strip[k : k + 1, :]
        lane = lax.broadcasted_iota(jnp.int32, (PANEL, wide), 1)
        line = lax.broadcasted_iota(jnp.int32, (PANEL, wide), 0)
        for leaf in range(per_device):
            strip = strips[leaf]
            pivots = jnp.sum(jnp.where(lane == line + start, strip, 0.0), axis=1, keepdims=True)
            strip = strip * (1.0 / jnp.sqrt(pivots))
            rows[leaf, start : start + PANEL, :] = strip
            if start + PANEL < red:
                work[leaf] = work[leaf] - matmul_t(strip[:, :red], strip, highest)
    for leaf in range(per_device):
        solved = rows[leaf, :, red : red + RANK]
        inverse = jnp.where(col_id <= row_id, rows[leaf, :, red + RANK :], 0.0)
        moved = matmul_t(inverse, solved, highest)
        shift[leaf] = moved.astype(jnp.bfloat16)
        turned = moved.T.astype(jnp.bfloat16)
        shift_t2[leaf, :, :red] = turned
        shift_t2[leaf, :, red:] = turned
    for leaf in range(per_device):
        solved = rows[leaf, :, red : red + RANK]
        panel[leaf] = solved
        skeleton[leaf] = low_corner[leaf] - matmul_t(solved, solved, highest)
        upper = jnp.where(col_id >= row_id, rows[leaf, :, :red], 0.0)
        factor[leaf] = upper.T


def window_kernel(
    chips,
    count,
    diag,
    bases,
    near,
    factor,
    panel,
    skeleton,
    shift_t2,
    halves,
    win_bases,
    win_shift,
    shift,
    bases_t,
    work,
    rows,
    near_in,
    half_out,
    send,
    recv,
    pass_send,
    pass_recv,
    own_sem,
    near_sem,
    half_sem,
):
    per_device, slots = near_in.shape[0], near_in.shape[1]
    fetches = [
        pltpu.make_async_copy(near.at[leaf], near_in.at[leaf], near_sem.at[leaf])
        for leaf in range(per_device)
    ]
    stores = [
        pltpu.make_async_copy(
            half_out.at[leaf], halves.at[leaf, pl.ds(0, slots)], half_sem.at[leaf]
        )
        for leaf in range(per_device)
    ]
    me = lax.axis_index("leaf")
    core = me % 2
    sibling = me + 1 - 2 * core
    offsets = [sign * step for step in range(chips, 0, -1) for sign in (1, -1)]
    pairs = ((bases, win_bases), (shift, win_shift))

    def inside(offset):
        other = me + 2 * offset
        return (other >= 0) & (other < count)

    barrier = pltpu.get_barrier_semaphore()
    pl.semaphore_signal(barrier, inc=1, device_id=(sibling,), device_id_type=MESH)
    for offset in offsets:

        @pl.when(inside(offset))
        def _(offset=offset):
            pl.semaphore_signal(barrier, inc=1, device_id=(me + 2 * offset,), device_id_type=MESH)

    peers = jnp.int32(1)
    for offset in offsets:
        peers = peers + inside(offset).astype(jnp.int32)
    pl.semaphore_wait(barrier, peers)

    def direct(kind, offset):
        source, window = pairs[kind]
        return pltpu.make_async_remote_copy(
            src_ref=source,
            dst_ref=window.at[2 * (chips - offset) + core],
            send_sem=send.at[kind, chips + offset],
            recv_sem=recv.at[kind, chips - offset],
            device_id=(me + 2 * offset,),
            device_id_type=MESH,
        )

    def arrival(kind, offset):
        source, window = pairs[kind]
        return pltpu.make_async_remote_copy(
            src_ref=source,
            dst_ref=window.at[2 * (chips + offset) + core],
            send_sem=send.at[kind, chips + offset],
            recv_sem=recv.at[kind, chips + offset],
            device_id=(sibling,),
            device_id_type=MESH,
        )

    def relay(kind, offset):
        source, window = pairs[kind]
        slot = 2 * (chips + offset) + core
        return pltpu.make_async_remote_copy(
            src_ref=source if offset == 0 else window.at[slot],
            dst_ref=window.at[slot],
            send_sem=pass_send.at[kind, chips + offset],
            recv_sem=pass_recv.at[kind, chips + offset],
            device_id=(sibling,),
            device_id_type=MESH,
        )

    def relayed(kind, offset):
        source, window = pairs[kind]
        slot = 2 * (chips + offset) + 1 - core
        return pltpu.make_async_remote_copy(
            src_ref=source,
            dst_ref=window.at[slot],
            send_sem=pass_send.at[kind, chips + offset],
            recv_sem=pass_recv.at[kind, chips + offset],
            device_id=(sibling,),
            device_id_type=MESH,
        )

    def dispatch(kind):
        for offset in offsets:

            @pl.when(inside(offset))
            def _(offset=offset):
                direct(kind, offset).start()

        relay(kind, 0).start()
        source, window = pairs[kind]
        pltpu.make_async_copy(source, window.at[2 * chips + core], own_sem.at[kind]).start()

    def hand_on(kind, offset):
        @pl.when(inside(offset))
        def _():
            arrival(kind, offset).wait_recv()
            relay(kind, offset).start()

    def project(first, last):
        @pl.loop(first, last)
        def _(n):
            for leaf in range(per_device):
                half_out[leaf, n] = matmul(bases_t[leaf], near_in[leaf, n]).astype(jnp.bfloat16)

    dispatch(0)
    for fetch in fetches:
        fetch.start()
    eliminate(diag, bases, factor, panel, skeleton, shift, shift_t2, bases_t, work, rows)
    dispatch(1)
    for fetch in fetches:
        fetch.wait()
    nearest = offsets[::-1]
    done = 0
    for turn, offset in enumerate(nearest):
        hand_on(0, offset)
        upto = slots * (turn + 1) // len(nearest)
        project(done, upto)
        done = upto
    for store in stores:
        store.start()
    for offset in nearest:
        hand_on(1, offset)

    for kind in range(2):
        source, window = pairs[kind]
        pltpu.make_async_copy(source, window.at[2 * chips + core], own_sem.at[kind]).wait()
        relay(kind, 0).wait_send()
        relayed(kind, 0).wait_recv()
        for offset in offsets:

            @pl.when(inside(offset))
            def _(kind=kind, offset=offset):
                direct(kind, offset).wait_send()
                relay(kind, offset).wait_send()
                relayed(kind, offset).wait_recv()

    for store in stores:
        store.wait()


def couple_kernel(
    chips,
    group,
    slots,
    where,
    nbrs,
    parents,
    halves,
    shift_t2,
    skeleton,
    win_bases,
    win_shift,
    merged,
    diagonal,
):
    leaf, step = pl.program_id(0), pl.program_id(1)
    per_device = pl.num_programs(0)
    steps = pl.num_programs(1)
    red = shift_t2.shape[2] // 2
    me = where[0]
    number = me * per_device + leaf
    parent = number // CHILDREN
    targets = parents.shape[1]

    @pl.when(step == 0)
    def _():
        merged[...] = jnp.zeros_like(merged)
        place = pl.multiple_of((number % CHILDREN) * RANK, RANK)
        for q in range(targets):

            @pl.when(parents[parent, q] == parent)
            def _(q=q):
                merged[0, q, :, pl.ds(place, RANK)] = skeleton[0]

    @pl.when(nbrs[leaf, step * group] >= 0)
    def _():
        results = []
        for k in range(group):
            n = step * group + k
            other = jnp.where(n < slots, nbrs[leaf, jnp.minimum(n, slots - 1)], -1)
            safe = jnp.where(other >= 0, other, number)
            owner = safe // per_device
            slot = (owner // 2 - me // 2 + chips) * 2 + owner % 2
            basis = win_bases[slot, safe % per_device]
            moved = win_shift[slot, safe % per_device]
            half = halves[0, k]
            right = matmul(half, basis[:, red:])
            left = matmul(half[red:], basis[:, :red])
            high = right[:red].astype(jnp.bfloat16)
            low = (right[:red] - high.astype(jnp.float32)).astype(jnp.bfloat16)
            first = matmul(shift_t2[0], jnp.concatenate([high, low], axis=0))
            high = left.astype(jnp.bfloat16)
            low = (left - high.astype(jnp.float32)).astype(jnp.bfloat16)
            second = matmul(
                jnp.concatenate([high, low], axis=1), jnp.concatenate([moved, moved], axis=0)
            )
            q = jnp.int32(-1)
            for place in range(targets):
                q = jnp.where(parents[parent, place] == safe // CHILDREN, place, q)
            results.append((right[red:] - first - second, other, q))
        for schur, other, q in results:

            @pl.when((other >= 0) & (q >= 0))
            def _(schur=schur, other=other, q=q):
                place = pl.multiple_of((other % CHILDREN) * RANK, RANK)
                merged[0, q, :, pl.ds(place, RANK)] = schur

    @pl.when(step == steps - 1)
    def _():
        diagonal[0] = merged[0, 0].astype(jnp.bfloat16)


def parent_kernel(size, own, diagonal, block, landed, send, recv):
    me = lax.axis_index("leaf")
    place = me % size
    base = me - place
    per_device, rank = own.shape[0], own.shape[2]
    width = per_device * rank
    barrier = pltpu.get_barrier_semaphore()
    for t in range(1, size):
        pl.semaphore_signal(
            barrier, inc=1, device_id=(base + (place + t) % size,), device_id_type=MESH
        )
    pl.semaphore_wait(barrier, size - 1)

    def copy(t):
        other = (place + t) % size
        return pltpu.make_async_remote_copy(
            src_ref=diagonal.at[:, :, pl.ds(pl.multiple_of(other * width, 128), width)],
            dst_ref=landed.at[size - t],
            send_sem=send.at[t],
            recv_sem=recv.at[size - t],
            device_id=(base + other,),
            device_id_type=MESH,
        )

    for t in range(1, size):
        copy(t).start()
    for t in range(size):
        other = (place + t) % size
        columns = pl.ds(pl.multiple_of(other * width, 128), width)
        mine = own[:, 0, :, columns].reshape(width, width)
        if t == 0:
            theirs = mine
        else:
            copy(size - t).wait_recv()
            theirs = landed[t].reshape(width, width).astype(jnp.float32)
        block[:, columns] = 0.5 * (mine + theirs.T)
    for t in range(1, size):
        copy(t).wait_send()


def local(count, near_blocks, diag_blocks, bases, leaf_nbrs, parent_nbrs):
    per_device, leaf_rows = bases.shape[0], bases.shape[1]
    red = leaf_rows - RANK
    slots = near_blocks.shape[1]
    targets = parent_nbrs.shape[1]
    span = REACH // per_device
    chips = (span + 1) // 2
    vmem = pl.BlockSpec(memory_space=pltpu.VMEM)
    anywhere = pl.BlockSpec(memory_space=pl.ANY)
    f32, bf16 = jnp.float32, jnp.bfloat16

    def out(shape, dtype):
        return jax.ShapeDtypeStruct(shape, dtype)

    group = 4
    steps = -(-slots // group)
    window = 2 * (2 * chips + 1)
    sems = pltpu.SemaphoreType.DMA((2, 2 * chips + 1))
    leaf_sems = pltpu.SemaphoreType.DMA((per_device,))
    factor, panel, skeleton, shift_t2, halves, win_bases, win_shift = pl.pallas_call(
        functools.partial(window_kernel, chips, count),
        out_shape=(
            out((per_device, red, red), f32),
            out((per_device, red, RANK), f32),
            out((per_device, RANK, RANK), f32),
            out((per_device, RANK, 2 * red), bf16),
            out((per_device, steps * group) + near_blocks.shape[2:], bf16),
            out((window,) + bases.shape, bf16),
            out((window, per_device, red, RANK), bf16),
        ),
        in_specs=[vmem, vmem, anywhere],
        out_specs=(vmem,) * 4 + (anywhere,) * 3,
        scratch_shapes=[
            pltpu.VMEM((per_device, red, RANK), bf16),
            pltpu.VMEM(bases.shape, bf16),
            pltpu.VMEM((per_device, red, 2 * red + RANK), f32),
            pltpu.VMEM((per_device, red, 2 * red + RANK), f32),
            pltpu.VMEM(near_blocks.shape, bf16),
            pltpu.VMEM(near_blocks.shape, bf16),
            sems,
            sems,
            sems,
            sems,
            pltpu.SemaphoreType.DMA((2,)),
            leaf_sems,
            leaf_sems,
        ],
        compiler_params=pltpu.CompilerParams(
            collective_id=0, has_side_effects=True, vmem_limit_bytes=66_000_000
        ),
        name="window",
    )(diag_blocks, bases, near_blocks)

    where = lax.axis_index("leaf").astype(jnp.int32).reshape(1)

    def half_map(leaf, step, where, nbrs, parents):
        return leaf, jnp.where(nbrs[leaf, step * group] >= 0, step, 0), 0, 0

    def by_leaf(rank):
        return lambda leaf, step, *_: (leaf,) + (0,) * (rank - 1)

    merged, diagonal = pl.pallas_call(
        functools.partial(couple_kernel, chips, group, slots),
        out_shape=(
            out((per_device, targets, RANK, CHILDREN * RANK), f32),
            out((per_device, RANK, CHILDREN * RANK), bf16),
        ),
        grid_spec=pltpu.PrefetchScalarGridSpec(
            num_scalar_prefetch=3,
            grid=(per_device, steps),
            in_specs=[
                pl.BlockSpec((1, group, leaf_rows, leaf_rows), half_map),
                pl.BlockSpec((1, RANK, 2 * red), by_leaf(3)),
                pl.BlockSpec((1, RANK, RANK), by_leaf(3)),
                vmem,
                vmem,
            ],
            out_specs=(
                pl.BlockSpec((1, targets, RANK, CHILDREN * RANK), by_leaf(4)),
                pl.BlockSpec((1, RANK, CHILDREN * RANK), by_leaf(3)),
            ),
        ),
        compiler_params=pltpu.CompilerParams(
            dimension_semantics=("arbitrary", "arbitrary"), vmem_limit_bytes=66_000_000
        ),
        name="couple",
    )(where, leaf_nbrs, parent_nbrs, halves, shift_t2, skeleton, win_bases, win_shift)

    size = CHILDREN // per_device
    width = per_device * RANK
    parent_block = pl.pallas_call(
        functools.partial(parent_kernel, size),
        out_shape=out((width, CHILDREN * RANK), f32),
        grid=(1,),
        in_specs=[
            pl.BlockSpec((per_device, 1, RANK, CHILDREN * RANK), lambda i: (0, 0, 0, 0)),
            vmem,
        ],
        out_specs=vmem,
        scratch_shapes=[
            pltpu.VMEM((size, per_device, RANK, width), bf16),
            pltpu.SemaphoreType.DMA((size,)),
            pltpu.SemaphoreType.DMA((size,)),
        ],
        compiler_params=pltpu.CompilerParams(collective_id=1, has_side_effects=True),
        name="parent",
    )(merged, diagonal)
    return factor, panel, merged, parent_block


def solution(mesh):
    count = mesh.shape["leaf"]
    in_specs = (
        P("leaf", None, None, None),
        P("leaf", None, None),
        P("leaf", None, None),
        P("leaf", None),
        P(),
    )
    out_specs = (
        P("leaf", None, None),
        P("leaf", None, None),
        P("leaf", None, None, None),
        P("leaf", None),
    )
    return jax.shard_map(
        functools.partial(local, count),
        mesh=mesh,
        in_specs=in_specs,
        out_specs=out_specs,
        check_vma=False,
    )
```

```python
import functools

import jax
import jax.numpy as jnp
from jax import lax
from jax.experimental import pallas as pl
from jax.experimental.pallas import tpu as pltpu
from jax.sharding import PartitionSpec as P

RANK = 128
REACH = 16
CHILDREN = 8
PANEL = 32
MESH = pl.DeviceIdType.MESH
highest = lax.Precision.HIGHEST


def matmul(a, b):
    return jnp.dot(a, b, preferred_element_type=jnp.float32)


def matmul_t(a, b, precision=None):
    return lax.dot_general(
        a, b, (((0,), (0,)), ((), ())), preferred_element_type=jnp.float32, precision=precision
    )


def eliminate(diag, bases, factor, panel, skeleton, shift, shift_t2, bases_t, work, rows):
    per_device, leaf_rows = bases.shape[0], bases.shape[1]
    red = leaf_rows - RANK
    wide = 2 * red + RANK
    row_id = lax.broadcasted_iota(jnp.int32, (red, red), 0)
    col_id = lax.broadcasted_iota(jnp.int32, (red, red), 1)
    low_corner = []
    for leaf in range(per_device):
        basis = bases[leaf]
        basis_t = basis.T
        bases_t[leaf] = basis_t
        half = matmul(basis_t, diag[leaf]).astype(jnp.bfloat16)
        dense = matmul(half, basis)
        top = dense[:red, :red]
        work[leaf, :, :red] = 0.5 * (top + top.T)
        work[leaf, :, red : red + RANK] = dense[:red, red:]
        work[leaf, :, red + RANK :] = (row_id == col_id).astype(jnp.float32)
        low_corner.append(dense[red:, red:])
    sub = lax.broadcasted_iota(jnp.int32, (PANEL, 1), 0)
    for start in range(0, red, PANEL):
        strips = [work[leaf, start : start + PANEL, :] for leaf in range(per_device)]
        for k in range(PANEL):
            for leaf in range(per_device):
                strip = strips[leaf]
                column = strip[:, start + k : start + k + 1]
                ratio = jnp.where(sub > k, column / column[k : k + 1], 0.0)
                strips[leaf] = strip - ratio * strip[k : k + 1, :]
        lane = lax.broadcasted_iota(jnp.int32, (PANEL, wide), 1)
        line = lax.broadcasted_iota(jnp.int32, (PANEL, wide), 0)
        for leaf in range(per_device):
            strip = strips[leaf]
            pivots = jnp.sum(jnp.where(lane == line + start, strip, 0.0), axis=1, keepdims=True)
            strip = strip * (1.0 / jnp.sqrt(pivots))
            rows[leaf, start : start + PANEL, :] = strip
            if start + PANEL < red:
                work[leaf] = work[leaf] - matmul_t(strip[:, :red], strip, highest)
    for leaf in range(per_device):
        solved = rows[leaf, :, red : red + RANK]
        inverse = jnp.where(col_id <= row_id, rows[leaf, :, red + RANK :], 0.0)
        moved = matmul_t(inverse, solved, highest)
        shift[leaf] = moved.astype(jnp.bfloat16)
        turned = moved.T.astype(jnp.bfloat16)
        shift_t2[leaf, :, :red] = turned
        shift_t2[leaf, :, red:] = turned
    for leaf in range(per_device):
        solved = rows[leaf, :, red : red + RANK]
        panel[leaf] = solved
        skeleton[leaf] = low_corner[leaf] - matmul_t(solved, solved, highest)
        upper = jnp.where(col_id >= row_id, rows[leaf, :, :red], 0.0)
        factor[leaf] = upper.T


def window_kernel(
    chips,
    count,
    diag,
    bases,
    near,
    factor,
    panel,
    skeleton,
    shift_t2,
    halves,
    win_bases,
    win_shift,
    shift,
    bases_t,
    work,
    rows,
    near_in,
    half_out,
    send,
    recv,
    pass_send,
    pass_recv,
    own_sem,
    near_sem,
    half_sem,
):
    per_device, slots = near_in.shape[0], near_in.shape[1]
    fetches = [
        pltpu.make_async_copy(near.at[leaf], near_in.at[leaf], near_sem.at[leaf])
        for leaf in range(per_device)
    ]
    stores = [
        pltpu.make_async_copy(
            half_out.at[leaf], halves.at[leaf, pl.ds(0, slots)], half_sem.at[leaf]
        )
        for leaf in range(per_device)
    ]
    me = lax.axis_index("leaf")
    core = me % 2
    sibling = me + 1 - 2 * core
    offsets = [sign * step for step in range(chips, 0, -1) for sign in (1, -1)]
    pairs = ((bases, win_bases), (shift, win_shift))

    def inside(offset):
        other = me + 2 * offset
        return (other >= 0) & (other < count)

    barrier = pltpu.get_barrier_semaphore()
    pl.semaphore_signal(barrier, inc=1, device_id=(sibling,), device_id_type=MESH)
    for offset in offsets:

        @pl.when(inside(offset))
        def _(offset=offset):
            pl.semaphore_signal(barrier, inc=1, device_id=(me + 2 * offset,), device_id_type=MESH)

    peers = jnp.int32(1)
    for offset in offsets:
        peers = peers + inside(offset).astype(jnp.int32)
    pl.semaphore_wait(barrier, peers)

    def direct(kind, offset):
        source, window = pairs[kind]
        return pltpu.make_async_remote_copy(
            src_ref=source,
            dst_ref=window.at[2 * (chips - offset) + core],
            send_sem=send.at[kind, chips + offset],
            recv_sem=recv.at[kind, chips - offset],
            device_id=(me + 2 * offset,),
            device_id_type=MESH,
        )

    def arrival(kind, offset):
        source, window = pairs[kind]
        return pltpu.make_async_remote_copy(
            src_ref=source,
            dst_ref=window.at[2 * (chips + offset) + core],
            send_sem=send.at[kind, chips + offset],
            recv_sem=recv.at[kind, chips + offset],
            device_id=(sibling,),
            device_id_type=MESH,
        )

    def relay(kind, offset):
        source, window = pairs[kind]
        slot = 2 * (chips + offset) + core
        return pltpu.make_async_remote_copy(
            src_ref=source if offset == 0 else window.at[slot],
            dst_ref=window.at[slot],
            send_sem=pass_send.at[kind, chips + offset],
            recv_sem=pass_recv.at[kind, chips + offset],
            device_id=(sibling,),
            device_id_type=MESH,
        )

    def relayed(kind, offset):
        source, window = pairs[kind]
        slot = 2 * (chips + offset) + 1 - core
        return pltpu.make_async_remote_copy(
            src_ref=source,
            dst_ref=window.at[slot],
            send_sem=pass_send.at[kind, chips + offset],
            recv_sem=pass_recv.at[kind, chips + offset],
            device_id=(sibling,),
            device_id_type=MESH,
        )

    def dispatch(kind):
        for offset in offsets:

            @pl.when(inside(offset))
            def _(offset=offset):
                direct(kind, offset).start()

        relay(kind, 0).start()
        source, window = pairs[kind]
        pltpu.make_async_copy(source, window.at[2 * chips + core], own_sem.at[kind]).start()

    def hand_on(kind, offset):
        @pl.when(inside(offset))
        def _():
            arrival(kind, offset).wait_recv()
            relay(kind, offset).start()

    def project(first, last):
        @pl.loop(first, last)
        def _(n):
            for leaf in range(per_device):
                half_out[leaf, n] = matmul(bases_t[leaf], near_in[leaf, n]).astype(jnp.bfloat16)

    dispatch(0)
    for fetch in fetches:
        fetch.start()
    eliminate(diag, bases, factor, panel, skeleton, shift, shift_t2, bases_t, work, rows)
    dispatch(1)
    for fetch in fetches:
        fetch.wait()
    done = 0
    for turn, offset in enumerate(offsets):
        hand_on(0, offset)
        upto = slots * (turn + 1) // len(offsets)
        project(done, upto)
        done = upto
    for store in stores:
        store.start()
    for offset in offsets:
        hand_on(1, offset)

    for kind in range(2):
        source, window = pairs[kind]
        pltpu.make_async_copy(source, window.at[2 * chips + core], own_sem.at[kind]).wait()
        relay(kind, 0).wait_send()
        relayed(kind, 0).wait_recv()
        for offset in offsets:

            @pl.when(inside(offset))
            def _(kind=kind, offset=offset):
                direct(kind, offset).wait_send()
                relay(kind, offset).wait_send()
                relayed(kind, offset).wait_recv()

    for store in stores:
        store.wait()


def neighbour(slots, nbrs, leaf, n):
    return jnp.where(n < slots, nbrs[leaf, jnp.minimum(n, slots - 1)], -1)


def couple_kernel(group, slots, where, nbrs, parents, halves, shift_t2, skeleton, *rest):
    win_bases, win_shift = rest[:group], rest[group : 2 * group]
    factor, panel, merged, diagonal, factor_out, panel_out = rest[2 * group :]
    leaf, step = pl.program_id(0), pl.program_id(1)
    per_device = pl.num_programs(0)
    steps = pl.num_programs(1)
    red = shift_t2.shape[2] // 2
    me = where[0]
    number = me * per_device + leaf
    parent = number // CHILDREN
    targets = parents.shape[1]

    @pl.when(step == 0)
    def _():
        merged[...] = jnp.zeros_like(merged)
        factor_out[...] = factor[...]
        panel_out[...] = panel[...]
        place = pl.multiple_of((number % CHILDREN) * RANK, RANK)
        for q in range(targets):

            @pl.when(parents[parent, q] == parent)
            def _(q=q):
                merged[0, q, :, pl.ds(place, RANK)] = skeleton[0]

    @pl.when(nbrs[leaf, step * group] >= 0)
    def _():
        results = []
        for k in range(group):
            other = neighbour(slots, nbrs, leaf, step * group + k)
            basis = win_bases[k][0, 0]
            moved = win_shift[k][0, 0]
            half = halves[0, k]
            right = matmul(half, basis[:, red:])
            left = matmul(half[red:], basis[:, :red])
            high = right[:red].astype(jnp.bfloat16)
            low = (right[:red] - high.astype(jnp.float32)).astype(jnp.bfloat16)
            first = matmul(shift_t2[0], jnp.concatenate([high, low], axis=0))
            high = left.astype(jnp.bfloat16)
            low = (left - high.astype(jnp.float32)).astype(jnp.bfloat16)
            second = matmul(
                jnp.concatenate([high, low], axis=1), jnp.concatenate([moved, moved], axis=0)
            )
            q = jnp.int32(-1)
            for place in range(targets):
                q = jnp.where(parents[parent, place] == other // CHILDREN, place, q)
            results.append((right[red:] - first - second, other, q))
        for schur, other, q in results:

            @pl.when((other >= 0) & (q >= 0))
            def _(schur=schur, other=other, q=q):
                place = pl.multiple_of((other % CHILDREN) * RANK, RANK)
                merged[0, q, :, pl.ds(place, RANK)] = schur

    @pl.when(step == steps - 1)
    def _():
        diagonal[0] = merged[0, 0].astype(jnp.bfloat16)


def parent_kernel(size, diagonal, landed, send, recv):
    me = lax.axis_index("leaf")
    place = me % size
    base = me - place
    width = landed.shape[3]
    barrier = pltpu.get_barrier_semaphore()
    for t in range(1, size):
        pl.semaphore_signal(
            barrier, inc=1, device_id=(base + (place + t) % size,), device_id_type=MESH
        )
    pl.semaphore_wait(barrier, size - 1)

    def copy(t, source):
        other = (place + t) % size
        return pltpu.make_async_remote_copy(
            src_ref=diagonal.at[:, :, pl.ds(pl.multiple_of(other * width, 128), width)],
            dst_ref=landed.at[source],
            send_sem=send.at[t],
            recv_sem=recv.at[size - t],
            device_id=(base + other,),
            device_id_type=MESH,
        )

    for t in range(1, size):
        copy(t, place).start()
    for t in range(1, size):
        copy(t, (place + size - t) % size).wait_recv()
    for t in range(1, size):
        copy(t, place).wait_send()


def symmetric_kernel(size, where, own, landed, block):
    width = block.shape[0]
    mine = own[:, 0].reshape(width, width)

    @pl.when(pl.program_id(0) == where[0] % size)
    def _():
        block[...] = 0.5 * (mine + mine.T)

    @pl.when(pl.program_id(0) != where[0] % size)
    def _():
        block[...] = 0.5 * (mine + landed[0].reshape(width, width).astype(jnp.float32).T)


def local(count, near_blocks, diag_blocks, bases, leaf_nbrs, parent_nbrs):
    per_device, leaf_rows = bases.shape[0], bases.shape[1]
    red = leaf_rows - RANK
    slots = near_blocks.shape[1]
    targets = parent_nbrs.shape[1]
    span = REACH // per_device
    chips = (span + 1) // 2
    vmem = pl.BlockSpec(memory_space=pltpu.VMEM)
    anywhere = pl.BlockSpec(memory_space=pl.ANY)
    f32, bf16 = jnp.float32, jnp.bfloat16

    def out(shape, dtype):
        return jax.ShapeDtypeStruct(shape, dtype)

    group = 4
    steps = -(-slots // group)
    window = 2 * (2 * chips + 1)
    sems = pltpu.SemaphoreType.DMA((2, 2 * chips + 1))
    leaf_sems = pltpu.SemaphoreType.DMA((per_device,))
    factor, panel, skeleton, shift_t2, halves, win_bases, win_shift = pl.pallas_call(
        functools.partial(window_kernel, chips, count),
        out_shape=(
            out((per_device, red, red), f32),
            out((per_device, red, RANK), f32),
            out((per_device, RANK, RANK), f32),
            out((per_device, RANK, 2 * red), bf16),
            out((per_device, steps * group) + near_blocks.shape[2:], bf16),
            out((window,) + bases.shape, bf16),
            out((window, per_device, red, RANK), bf16),
        ),
        in_specs=[vmem, vmem, anywhere],
        out_specs=(vmem,) * 4 + (anywhere,) * 3,
        scratch_shapes=[
            pltpu.VMEM((per_device, red, RANK), bf16),
            pltpu.VMEM(bases.shape, bf16),
            pltpu.VMEM((per_device, red, 2 * red + RANK), f32),
            pltpu.VMEM((per_device, red, 2 * red + RANK), f32),
            pltpu.VMEM(near_blocks.shape, bf16),
            pltpu.VMEM(near_blocks.shape, bf16),
            sems,
            sems,
            sems,
            sems,
            pltpu.SemaphoreType.DMA((2,)),
            leaf_sems,
            leaf_sems,
        ],
        compiler_params=pltpu.CompilerParams(
            collective_id=0, has_side_effects=True, vmem_limit_bytes=66_000_000
        ),
        name="window",
    )(diag_blocks, bases, near_blocks)

    where = lax.axis_index("leaf").astype(jnp.int32).reshape(1)

    def half_map(leaf, step, where, nbrs, parents):
        return leaf, jnp.where(nbrs[leaf, step * group] >= 0, step, 0), 0, 0

    def window_map(k):
        def index(leaf, step, where, nbrs, parents):
            me = where[0]
            other = neighbour(slots, nbrs, leaf, step * group + k)
            other = jnp.where(other >= 0, other, me * per_device + leaf)
            owner = other // per_device
            slot = (owner // 2 - me // 2 + chips) * 2 + owner % 2
            return slot, other % per_device, 0, 0

        return index

    def by_leaf(rank):
        return lambda leaf, step, *_: (leaf,) + (0,) * (rank - 1)

    merged, diagonal, factor, panel = pl.pallas_call(
        functools.partial(couple_kernel, group, slots),
        out_shape=(
            out((per_device, targets, RANK, CHILDREN * RANK), f32),
            out((per_device, RANK, CHILDREN * RANK), bf16),
            out(factor.shape, f32),
            out(panel.shape, f32),
        ),
        grid_spec=pltpu.PrefetchScalarGridSpec(
            num_scalar_prefetch=3,
            grid=(per_device, steps),
            in_specs=[
                pl.BlockSpec((1, group, leaf_rows, leaf_rows), half_map),
                pl.BlockSpec((1, RANK, 2 * red), by_leaf(3)),
                pl.BlockSpec((1, RANK, RANK), by_leaf(3)),
            ]
            + [pl.BlockSpec((1, 1, leaf_rows, leaf_rows), window_map(k)) for k in range(group)]
            + [pl.BlockSpec((1, 1, red, RANK), window_map(k)) for k in range(group)]
            + [
                pl.BlockSpec((1, red, red), by_leaf(3)),
                pl.BlockSpec((1, red, RANK), by_leaf(3)),
            ],
            out_specs=(
                pl.BlockSpec((1, targets, RANK, CHILDREN * RANK), by_leaf(4)),
                pl.BlockSpec((1, RANK, CHILDREN * RANK), by_leaf(3)),
                pl.BlockSpec((1, red, red), by_leaf(3)),
                pl.BlockSpec((1, red, RANK), by_leaf(3)),
            ),
        ),
        compiler_params=pltpu.CompilerParams(
            dimension_semantics=("arbitrary", "arbitrary"), vmem_limit_bytes=66_000_000
        ),
        name="couple",
    )(
        where,
        leaf_nbrs,
        parent_nbrs,
        halves,
        shift_t2,
        skeleton,
        *[win_bases] * group,
        *[win_shift] * group,
        factor,
        panel,
    )

    size = CHILDREN // per_device
    width = per_device * RANK
    landed = pl.pallas_call(
        functools.partial(parent_kernel, size),
        out_shape=out((size, per_device, RANK, width), bf16),
        in_specs=[anywhere],
        out_specs=anywhere,
        scratch_shapes=[
            pltpu.SemaphoreType.DMA((size,)),
            pltpu.SemaphoreType.DMA((size,)),
        ],
        compiler_params=pltpu.CompilerParams(
            collective_id=1, has_side_effects=True, vmem_limit_bytes=66_000_000
        ),
        name="parent",
    )(diagonal)

    parent_block = pl.pallas_call(
        functools.partial(symmetric_kernel, size),
        out_shape=out((width, CHILDREN * RANK), f32),
        grid_spec=pltpu.PrefetchScalarGridSpec(
            num_scalar_prefetch=1,
            grid=(size,),
            in_specs=[
                pl.BlockSpec((per_device, 1, RANK, width), lambda t, *_: (0, 0, 0, t)),
                pl.BlockSpec((1, per_device, RANK, width), lambda t, *_: (t, 0, 0, 0)),
            ],
            out_specs=pl.BlockSpec((width, width), lambda t, *_: (0, t)),
        ),
        compiler_params=pltpu.CompilerParams(vmem_limit_bytes=66_000_000),
        name="symmetric",
    )(where, merged, landed)
    return factor, panel, merged, parent_block


def solution(mesh):
    count = mesh.shape["leaf"]
    in_specs = (
        P("leaf", None, None, None),
        P("leaf", None, None),
        P("leaf", None, None),
        P("leaf", None),
        P(),
    )
    out_specs = (
        P("leaf", None, None),
        P("leaf", None, None),
        P("leaf", None, None, None),
        P("leaf", None),
    )
    return jax.shard_map(
        functools.partial(local, count),
        mesh=mesh,
        in_specs=in_specs,
        out_specs=out_specs,
        check_vma=False,
    )
```
